128 devices in a mesh: lists: 8 (over z, core), seq: 16 (over y, x).
Axes of the slice: x: 4, y: 4, z: 4, core: 2. Of those that a mesh axis runs over, the one named last changes fastest.
Arguments:
- queries: bfloat16 [98304, 2048], P(('lists', 'seq')), parts along dimension 0, may hold values from -6 to 6
- key_rows: bfloat16 [98304, 2048], P(('lists', 'seq')), parts along dimension 0, may hold values from -6 to 6
- value_rows: bfloat16 [98304, 2048], P(('lists', 'seq')), parts along dimension 0, may hold values from -6 to 6
- out_grad: bfloat16 [98304, 2048], P(('lists', 'seq')), parts along dimension 0, may hold values from -6 to 6
Outputs:
- query_grad: bfloat16 [98304, 2048], P(('lists', 'seq')), parts along dimension 0
- key_grad: bfloat16 [98304, 2048], P(('lists', 'seq')), parts along dimension 0
- content_derivative: bfloat16 [98304, 2048], P(('lists', 'seq')), parts along dimension 0
The draws below stay inside these ranges and needn't reach their ends.
There are 8 independent parts, one for each index of `lists`. The reference program is written for one: setup_inputs(seed, part) draws one part's arguments, and reference() takes and returns one part's arrays. A program takes and returns all parts, laid end to end along the dimension named above; each array names one. Nothing has to cross between parts.
All inputs are finite; a program needn't handle non-finite values.
Results may differ from the reference program's by a relative error of at most 0.0049.
Values sent between devices are 32-bit elements; how exact they have to be, the bound alone decides.
A program may use at most 192 MiB of HBM per device.

```python
import jax
import jax.numpy as jnp
from jax import lax

HEADS = 16
HEAD_DIM = 128
TOK_DEV = 768
WIDTH = 2048
LENGTH = 12288


def block_levels(stream_key, dims, cuts, least, high):
    def one(dim, shards_of):
        draws = jax.random.uniform(jax.random.fold_in(jax.random.fold_in(stream_key, 6), dim), (shards_of,), jnp.float32, least / len(cuts), high / len(cuts))
        return jnp.repeat(jnp.exp(draws), dims[dim] // shards_of).reshape((-1,) + (1,) * (len(dims) - dim - 1))

    factor_of = one(*cuts[0])
    for cut in cuts[1:]:
        factor_of = factor_of * one(*cut)
    return factor_of


def bell_draw(own_key, extent, spread, reach, split=(), kind=jnp.bfloat16):
    factor_of = block_levels(own_key, extent, split, -0.22, 0.18) if split else 1.0
    result = jax.random.normal(own_key, extent, jnp.float32) * spread * factor_of
    return jnp.minimum(jnp.maximum(result, -reach), reach).astype(kind)


def setup_inputs(seed: int = 0, part: int = 0) -> dict:
    key_of = jax.random.split(jax.random.key(seed), 5)
    part_splits = jax.random.split(jax.random.fold_in(key_of[4], part), 5)
    return {
        "queries": bell_draw(part_splits[0], (LENGTH, WIDTH), 1.0, 6.0, ((0, 16),)),
        "key_rows": bell_draw(part_splits[1], (LENGTH, WIDTH), 1.0, 6.0, ((0, 16),)),
        "value_rows": bell_draw(part_splits[2], (LENGTH, WIDTH), 1.0, 6.0, ((0, 16),)),
        "out_grad": bell_draw(part_splits[3], (LENGTH, WIDTH), 1.0, 6.0, ((0, 16),)),
    }


def reference(queries, key_rows, value_rows, out_grad):
    blocks = LENGTH // TOK_DEV
    scale_factor = (HEAD_DIM * LENGTH) ** -0.5
    dimensions_4 = (blocks, TOK_DEV, HEADS, HEAD_DIM)
    query_blocks = queries.reshape(dimensions_4)
    lookup_segments = key_rows.reshape(dimensions_4)
    value_blocks = value_rows.reshape(dimensions_4)
    grad_blocks = out_grad.reshape(dimensions_4)
    key_value_sum = jnp.einsum('bshk,bshv->bhkv', lookup_segments.astype(jnp.float32), value_blocks.astype(jnp.float32))
    query_output_sum = jnp.einsum('bthk,bthv->bhkv', query_blocks.astype(jnp.float32), grad_blocks.astype(jnp.float32))
    zero_state = jnp.zeros((1, HEADS, HEAD_DIM, HEAD_DIM), jnp.float32)
    cumulative_leading = jnp.concatenate([zero_state, jnp.cumsum(key_value_sum, axis=0)[:-1]], axis=0).astype(jnp.bfloat16)
    reverse_sum = jnp.cumsum(query_output_sum[::-1], axis=0)[::-1]
    suffix = jnp.concatenate([reverse_sum[1:], zero_state], axis=0).astype(jnp.bfloat16)
    later = jnp.arange(TOK_DEV, dtype=jnp.int32)
    causal = later[:, None] >= later[None, :]

    def one_block(items):
        query_one, key_one, value_one, grad_one, prefix_one, suffix_one = items
        query_float = query_one.astype(jnp.float32)
        key_float = key_one.astype(jnp.float32)
        value_float = value_one.astype(jnp.float32)
        gradient_float = grad_one.astype(jnp.float32)
        scores = jnp.einsum('thk,shk->hts', query_float, key_float)
        forward_weight_matrix = jnp.where(causal[None], scale_factor * scores, 0.0).astype(jnp.bfloat16).astype(jnp.float32)
        products = jnp.einsum('thv,shv->hts', gradient_float, value_float)
        weight_gradients = jnp.where(causal[None], scale_factor * products, 0.0).astype(jnp.bfloat16).astype(jnp.float32)
        prefix_float = prefix_one.astype(jnp.float32)
        suffix_float = suffix_one.astype(jnp.float32)
        query_portion = jnp.einsum('ynv,vyq->nyq', weight_gradients, key_float) + scale_factor * jnp.einsum('aro,rbo->arb', gradient_float, prefix_float)
        key_portion = jnp.einsum('eca,ceo->aeo', weight_gradients, query_float) + scale_factor * jnp.einsum('jan,aon->jao', value_float, suffix_float)
        value_portion = jnp.einsum('uno,nud->oud', forward_weight_matrix, gradient_float) + scale_factor * jnp.einsum('nam,amx->nax', key_float, suffix_float)
        return (query_portion.astype(jnp.bfloat16), key_portion.astype(jnp.bfloat16), value_portion.astype(jnp.bfloat16))

    query_grad, key_grad, content_derivative = lax.map(one_block, (query_blocks, lookup_segments, value_blocks, grad_blocks, cumulative_leading, suffix))
    flat = (LENGTH, HEADS * HEAD_DIM)
    return (query_grad.reshape(flat), key_grad.reshape(flat), content_derivative.reshape(flat))
```

```python
import functools

import jax
import jax.numpy as jnp
from jax import lax
from jax.experimental import pallas as pl
from jax.experimental.pallas import tpu as pltpu
from jax.sharding import PartitionSpec as P

HEADS = 16
HEAD_DIM = 128
CHUNK = 256
MESH = pl.DeviceIdType.MESH
F32 = jnp.float32
BF16 = jnp.bfloat16


def mm(a, b):
    return lax.dot_general(a, b, (((1,), (0,)), ((), ())), preferred_element_type=F32)


def mm_nt(a, b):
    return lax.dot_general(a, b, (((1,), (1,)), ((), ())), preferred_element_type=F32)


def mm_tn(a, b):
    return lax.dot_general(a, b, (((0,), (0,)), ((), ())), preferred_element_type=F32)


def kernel(
    scale,
    count,
    early,
    q_hbm,
    k_hbm,
    v_hbm,
    g_hbm,
    dq_ref,
    dk_ref,
    dv_ref,
    q_ref,
    k_ref,
    v_ref,
    g_ref,
    pq_ref,
    pk_ref,
    pv_ref,
    sums,
    parts,
    gathered,
    scans,
    states,
    load_sem,
    send_a,
    recv_a,
    send_b,
    recv_b,
):
    me = lax.axis_index("seq")
    rows = q_ref.shape[0]
    chunks = rows // CHUNK

    def peer(step):
        return lax.rem(me + step, count)

    def lanes(head):
        return pl.ds(pl.multiple_of(head * HEAD_DIM, HEAD_DIM), HEAD_DIM)

    barrier = pltpu.get_barrier_semaphore()

    def greet(step, carry):
        pl.semaphore_signal(barrier, inc=1, device_id={"seq": peer(step)}, device_id_type=MESH)
        return carry

    lax.fori_loop(1, count, greet, 0)

    def load(which, head):
        source = (k_hbm, v_hbm, q_hbm, g_hbm)[which]
        target = (k_ref, v_ref, q_ref, g_ref)[which]
        return pltpu.make_async_copy(
            source.at[:, lanes(head)], target.at[:, lanes(head)], load_sem.at[which, head]
        )

    for pair in ((0, 1), (2, 3)):

        def begin(step, carry):
            for which in pair:
                load(which, peer(step)).start()
            return carry

        lax.fori_loop(1, count + 1, begin, 0)

    def to_hub(kind, head):
        return pltpu.make_async_remote_copy(
            src_ref=sums.at[kind, head],
            dst_ref=gathered.at[kind, me],
            send_sem=send_a.at[kind, head],
            recv_sem=recv_a.at[kind, me],
            device_id={"seq": head},
            device_id_type=MESH,
        )

    def from_source(kind, source):
        return pltpu.make_async_remote_copy(
            src_ref=sums.at[kind, source],
            dst_ref=gathered.at[kind, source],
            send_sem=send_a.at[kind, source],
            recv_sem=recv_a.at[kind, source],
            device_id={"seq": source},
            device_id_type=MESH,
        )

    def to_owner(kind, owner):
        return pltpu.make_async_remote_copy(
            src_ref=scans.at[kind, owner],
            dst_ref=states.at[kind, me],
            send_sem=send_b.at[kind, owner],
            recv_sem=recv_b.at[kind, me],
            device_id={"seq": owner},
            device_id_type=MESH,
        )

    def from_hub(kind, hub):
        return pltpu.make_async_remote_copy(
            src_ref=scans.at[kind, hub],
            dst_ref=states.at[kind, hub],
            send_sem=send_b.at[kind, hub],
            recv_sem=recv_b.at[kind, hub],
            device_id={"seq": hub},
            device_id_type=MESH,
        )

    def reduce_head(kind, head):
        left = (k_ref, q_ref)[kind]
        right = (v_ref, g_ref)[kind]
        for which in ((0, 1), (2, 3))[kind]:
            load(which, head).wait()
        total = None
        for step in range(chunks):
            chunk = step if kind == 0 else chunks - 1 - step
            here = pl.ds(chunk * CHUNK, CHUNK)
            term = mm_tn(left[here, lanes(head)], right[here, lanes(head)])
            total = term if total is None else total + term
            if step < chunks - 1:
                parts[kind, step, head] = total
        return total

    for kind in (0, 1):
        if kind == 0:
            head = peer(1)
            sums[kind, head] = reduce_head(kind, head)
            pl.semaphore_wait(barrier, count - 1)
            to_hub(kind, head).start()

        def send_sums(step, carry):
            head = peer(step)
            sums[kind, head] = reduce_head(kind, head)
            to_hub(kind, head).start()
            return carry

        lax.fori_loop(2 - kind, count, send_sums, 0)
        gathered[kind, me] = reduce_head(kind, me)

    later = lax.broadcasted_iota(jnp.int32, (CHUNK, CHUNK), 0)
    sooner = lax.broadcasted_iota(jnp.int32, (CHUNK, CHUNK), 1)

    def within(head, carry):
        for chunk in range(chunks):
            here = pl.ds(chunk * CHUNK, CHUNK)
            q = q_ref[here, lanes(head)]
            k = k_ref[here, lanes(head)]
            v = v_ref[here, lanes(head)]
            g = g_ref[here, lanes(head)]
            weights = jnp.where(later >= sooner, scale * mm_nt(g, v), 0.0).astype(BF16)
            pq_ref[here, lanes(head)] = mm(weights, k)
            turned = jnp.where(later <= sooner, scale * mm_nt(v, g), 0.0).astype(BF16)
            pk_ref[here, lanes(head)] = mm(turned, q)
            forward = jnp.where(later <= sooner, scale * mm_nt(k, q), 0.0).astype(BF16)
            pv_ref[here, lanes(head)] = mm(forward, g)
        return carry

    def scan(kind):
        def arrive(step, carry):
            from_source(kind, peer(step)).wait_recv()
            return carry

        lax.fori_loop(1, count, arrive, 0)

        def add(step, carry):
            source = step if kind == 0 else count - 1 - step
            scans[kind, source] = carry
            return carry + gathered[kind, source]

        lax.fori_loop(0, count, add, jnp.zeros((HEAD_DIM, HEAD_DIM), F32))
        states[kind, me] = scans[kind, me]

        def give(step, carry):
            to_owner(kind, peer(step)).start()
            return carry

        lax.fori_loop(1, count, give, 0)

    lax.fori_loop(0, early, within, 0)
    scan(0)
    lax.fori_loop(early, HEADS, within, 0)
    scan(1)

    def state_at(kind, head, step):
        state = states[kind, head]
        if step > 0:
            state = state + parts[kind, step - 1, head]
        return state.astype(BF16)

    def finish_q(head):
        for chunk in range(chunks):
            here = pl.ds(chunk * CHUNK, CHUNK)
            carried = mm_nt(g_ref[here, lanes(head)], state_at(0, head, chunk))
            dq_ref[here, lanes(head)] = (pq_ref[here, lanes(head)] + scale * carried).astype(BF16)

    def finish_kv(head):
        for chunk in range(chunks):
            here = pl.ds(chunk * CHUNK, CHUNK)
            state = state_at(1, head, chunks - 1 - chunk)
            carried = mm_nt(v_ref[here, lanes(head)], state)
            dk_ref[here, lanes(head)] = (pk_ref[here, lanes(head)] + scale * carried).astype(BF16)
            carried = mm(k_ref[here, lanes(head)], state)
            dv_ref[here, lanes(head)] = (pv_ref[here, lanes(head)] + scale * carried).astype(BF16)

    for kind, finish in ((0, finish_q), (1, finish_kv)):
        finish(me)

        def settle(step, carry):
            head = peer(count - step)
            from_hub(kind, head).wait_recv()
            finish(head)
            return carry

        lax.fori_loop(1, count, settle, 0)

    for kind in (0, 1):

        def sent(step, carry):
            to_hub(kind, peer(step)).wait_send()
            to_owner(kind, peer(step)).wait_send()
            return carry

        lax.fori_loop(1, count, sent, 0)


def on_device(queries, key_rows, value_rows, out_grad):
    rows, width = queries.shape
    count = lax.axis_size("seq")
    scale = (HEAD_DIM * rows * count) ** (-0.5)
    wide = (rows, width)
    square = (HEAD_DIM, HEAD_DIM)
    chunks = rows // CHUNK
    return pl.pallas_call(
        functools.partial(kernel, scale, count, 10),
        name="layer",
        out_shape=[OUT(wide, BF16)] * 3,
        in_specs=[pl.BlockSpec(memory_space=pl.ANY)] * 4,
        out_specs=[pl.BlockSpec(memory_space=pltpu.VMEM)] * 3,
        scratch_shapes=[pltpu.VMEM(wide, BF16)] * 4
        + [pltpu.VMEM(wide, F32)] * 3
        + [
            pltpu.VMEM((2, HEADS) + square, F32),
            pltpu.VMEM((2, chunks - 1, HEADS) + square, F32),
            pltpu.VMEM((2, count) + square, F32),
            pltpu.VMEM((2, count) + square, F32),
            pltpu.VMEM((2, HEADS) + square, F32),
            pltpu.SemaphoreType.DMA((4, HEADS)),
            pltpu.SemaphoreType.DMA((2, HEADS)),
            pltpu.SemaphoreType.DMA((2, count)),
            pltpu.SemaphoreType.DMA((2, count)),
            pltpu.SemaphoreType.DMA((2, HEADS)),
        ],
        compiler_params=pltpu.CompilerParams(
            collective_id=0, has_side_effects=True, vmem_limit_bytes=62 << 20
        ),
    )(queries, key_rows, value_rows, out_grad)


OUT = jax.ShapeDtypeStruct


def solution(mesh):
    placed = P(("lists", "seq"), None)
    return jax.shard_map(
        on_device,
        mesh=mesh,
        in_specs=(placed,) * 4,
        out_specs=(placed,) * 3,
        check_vma=False,
    )
```

```python
import functools

import jax
import jax.numpy as jnp
from jax import lax
from jax.experimental import pallas as pl
from jax.experimental.pallas import tpu as pltpu
from jax.sharding import PartitionSpec as P

HEADS = 16
HEAD_DIM = 128
CHUNK = 256
MESH = pl.DeviceIdType.MESH
F32 = jnp.float32
BF16 = jnp.bfloat16


def mm(a, b):
    return lax.dot_general(a, b, (((1,), (0,)), ((), ())), preferred_element_type=F32)


def mm_nt(a, b):
    return lax.dot_general(a, b, (((1,), (1,)), ((), ())), preferred_element_type=F32)


def mm_tn(a, b):
    return lax.dot_general(a, b, (((0,), (0,)), ((), ())), preferred_element_type=F32)


def kernel(
    scale,
    count,
    early,
    q_hbm,
    k_hbm,
    v_hbm,
    g_hbm,
    dq_ref,
    dk_ref,
    dv_ref,
    q_ref,
    k_ref,
    v_ref,
    g_ref,
    pq_ref,
    pk_ref,
    pv_ref,
    sums,
    parts,
    gathered,
    scans,
    states,
    load_sem,
    send_a,
    recv_a,
    send_b,
    recv_b,
):
    me = lax.axis_index("seq")
    rows = q_ref.shape[0]
    chunks = rows // CHUNK

    def peer(step):
        return lax.rem(me + step, count)

    def lanes(head):
        return pl.ds(pl.multiple_of(head * HEAD_DIM, HEAD_DIM), HEAD_DIM)

    barrier = pltpu.get_barrier_semaphore()

    def greet(step, carry):
        pl.semaphore_signal(barrier, inc=1, device_id={"seq": peer(step)}, device_id_type=MESH)
        return carry

    lax.fori_loop(1, count, greet, 0)

    def pair_at(step):
        return lax.rem(me // 2 + step, HEADS // 2)

    def wide_lanes(pair):
        return pl.ds(pl.multiple_of(pair * 2 * HEAD_DIM, 2 * HEAD_DIM), 2 * HEAD_DIM)

    def load(which, pair):
        source = (k_hbm, v_hbm, q_hbm, g_hbm)[which]
        target = (k_ref, v_ref, q_ref, g_ref)[which]
        return pltpu.make_async_copy(
            source.at[:, wide_lanes(pair)], target.at[:, wide_lanes(pair)], load_sem.at[which, pair]
        )

    for first in (0, 2):

        def begin(step, carry):
            load(first, pair_at(step)).start()
            load(first + 1, pair_at(step)).start()
            return carry

        lax.fori_loop(1, HEADS // 2 + 1, begin, 0)

    def to_hub(kind, head):
        return pltpu.make_async_remote_copy(
            src_ref=sums.at[kind, head],
            dst_ref=gathered.at[kind, me],
            send_sem=send_a.at[kind, head],
            recv_sem=recv_a.at[kind, me],
            device_id={"seq": head},
            device_id_type=MESH,
        )

    def from_source(kind, source):
        return pltpu.make_async_remote_copy(
            src_ref=sums.at[kind, source],
            dst_ref=gathered.at[kind, source],
            send_sem=send_a.at[kind, source],
            recv_sem=recv_a.at[kind, source],
            device_id={"seq": source},
            device_id_type=MESH,
        )

    def to_owner(kind, owner):
        return pltpu.make_async_remote_copy(
            src_ref=scans.at[kind, owner],
            dst_ref=states.at[kind, me],
            send_sem=send_b.at[kind, owner],
            recv_sem=recv_b.at[kind, me],
            device_id={"seq": owner},
            device_id_type=MESH,
        )

    def from_hub(kind, hub):
        return pltpu.make_async_remote_copy(
            src_ref=scans.at[kind, hub],
            dst_ref=states.at[kind, hub],
            send_sem=send_b.at[kind, hub],
            recv_sem=recv_b.at[kind, hub],
            device_id={"seq": hub},
            device_id_type=MESH,
        )

    def reduce_pair(kind, pair):
        left = (k_ref, q_ref)[kind]
        right = (v_ref, g_ref)[kind]
        load(2 * kind, pair).wait()
        load(2 * kind + 1, pair).wait()
        total = None
        for step in range(chunks):
            chunk = step if kind == 0 else chunks - 1 - step
            here = pl.ds(chunk * CHUNK, CHUNK)
            both = mm_tn(left[here, wide_lanes(pair)], right[here, wide_lanes(pair)])
            term = (both[:HEAD_DIM, :HEAD_DIM], both[HEAD_DIM:, HEAD_DIM:])
            total = term if total is None else (total[0] + term[0], total[1] + term[1])
            for one in (0, 1):
                if step < chunks - 1:
                    parts[kind, step, 2 * pair + one] = total[one]
                else:
                    sums[kind, 2 * pair + one] = total[one]

    for kind in (0, 1):

        def send_sums(step, carry):
            pair = pair_at(step)
            reduce_pair(kind, pair)
            if kind == 0:

                @pl.when(step == 1)
                def _():
                    pl.semaphore_wait(barrier, count - 1)

            for one in (0, 1):
                head = 2 * pair + one

                @pl.when(head != me)
                def _():
                    to_hub(kind, head).start()

            return carry

        lax.fori_loop(1, HEADS // 2 + 1, send_sums, 0)
        gathered[kind, me] = sums[kind, me]

    later = lax.broadcasted_iota(jnp.int32, (CHUNK, CHUNK), 0)
    sooner = lax.broadcasted_iota(jnp.int32, (CHUNK, CHUNK), 1)

    def within(head, carry):
        for chunk in range(chunks):
            here = pl.ds(chunk * CHUNK, CHUNK)
            q = q_ref[here, lanes(head)]
            k = k_ref[here, lanes(head)]
            v = v_ref[here, lanes(head)]
            g = g_ref[here, lanes(head)]
            weights = jnp.where(later >= sooner, scale * mm_nt(g, v), 0.0).astype(BF16)
            pq_ref[here, lanes(head)] = mm(weights, k)
            turned = jnp.where(later <= sooner, scale * mm_nt(v, g), 0.0).astype(BF16)
            pk_ref[here, lanes(head)] = mm(turned, q)
            forward = jnp.where(later <= sooner, scale * mm_nt(k, q), 0.0).astype(BF16)
            pv_ref[here, lanes(head)] = mm(forward, g)
        return carry

    def scan(kind):
        def arrive(step, carry):
            from_source(kind, peer(step)).wait_recv()
            return carry

        lax.fori_loop(1, count, arrive, 0)

        def add(step, carry):
            source = step if kind == 0 else count - 1 - step
            scans[kind, source] = carry
            return carry + gathered[kind, source]

        lax.fori_loop(0, count, add, jnp.zeros((HEAD_DIM, HEAD_DIM), F32))
        states[kind, me] = scans[kind, me]

        def give(step, carry):
            to_owner(kind, peer(step)).start()
            return carry

        lax.fori_loop(1, count, give, 0)

    lax.fori_loop(0, early, within, 0)
    scan(0)
    lax.fori_loop(early, HEADS, within, 0)
    scan(1)

    def state_at(kind, head, step):
        state = states[kind, head]
        if step > 0:
            state = state + parts[kind, step - 1, head]
        return state.astype(BF16)

    def finish_q(head):
        for chunk in range(chunks):
            here = pl.ds(chunk * CHUNK, CHUNK)
            carried = mm_nt(g_ref[here, lanes(head)], state_at(0, head, chunk))
            dq_ref[here, lanes(head)] = (pq_ref[here, lanes(head)] + scale * carried).astype(BF16)

    def finish_kv(head):
        for chunk in range(chunks):
            here = pl.ds(chunk * CHUNK, CHUNK)
            state = state_at(1, head, chunks - 1 - chunk)
            carried = mm_nt(v_ref[here, lanes(head)], state)
            dk_ref[here, lanes(head)] = (pk_ref[here, lanes(head)] + scale * carried).astype(BF16)
            carried = mm(k_ref[here, lanes(head)], state)
            dv_ref[here, lanes(head)] = (pv_ref[here, lanes(head)] + scale * carried).astype(BF16)

    for kind, finish in ((0, finish_q), (1, finish_kv)):
        finish(me)

        def settle(step, carry):
            head = peer(count - step)
            from_hub(kind, head).wait_recv()
            finish(head)
            return carry

        lax.fori_loop(1, count, settle, 0)

    for kind in (0, 1):

        def sent(step, carry):
            to_hub(kind, peer(step)).wait_send()
            to_owner(kind, peer(step)).wait_send()
            return carry

        lax.fori_loop(1, count, sent, 0)


def on_device(queries, key_rows, value_rows, out_grad):
    rows, width = queries.shape
    count = lax.axis_size("seq")
    scale = (HEAD_DIM * rows * count) ** (-0.5)
    wide = (rows, width)
    square = (HEAD_DIM, HEAD_DIM)
    chunks = rows // CHUNK
    return pl.pallas_call(
        functools.partial(kernel, scale, count, 10),
        name="layer",
        out_shape=[pltpu.VMEM(wide, BF16)] * 3,
        in_specs=[pl.BlockSpec(memory_space=pl.ANY)] * 4,
        out_specs=[pl.BlockSpec(memory_space=pltpu.VMEM)] * 3,
        scratch_shapes=[pltpu.VMEM(wide, BF16)] * 4
        + [pltpu.VMEM(wide, F32)] * 3
        + [
            pltpu.VMEM((2, HEADS) + square, F32),
            pltpu.VMEM((2, chunks - 1, HEADS) + square, F32),
            pltpu.VMEM((2, count) + square, F32),
            pltpu.VMEM((2, count) + square, F32),
            pltpu.VMEM((2, HEADS) + square, F32),
            pltpu.SemaphoreType.DMA((4, HEADS)),
            pltpu.SemaphoreType.DMA((2, HEADS)),
            pltpu.SemaphoreType.DMA((2, count)),
            pltpu.SemaphoreType.DMA((2, count)),
            pltpu.SemaphoreType.DMA((2, HEADS)),
        ],
        compiler_params=pltpu.CompilerParams(
            collective_id=0, has_side_effects=True, vmem_limit_bytes=48 << 20
        ),
    )(queries, key_rows, value_rows, out_grad)


def solution(mesh):
    placed = P(("lists", "seq"), None)
    return jax.shard_map(
        on_device,
        mesh=mesh,
        in_specs=(placed,) * 4,
        out_specs=(placed,) * 3,
        check_vma=False,
    )
```

```python
import functools

import jax
import jax.numpy as jnp
from jax import lax
from jax.experimental import pallas as pl
from jax.experimental.pallas import tpu as pltpu
from jax.sharding import PartitionSpec as P

HEADS = 16
HEAD_DIM = 128
CHUNK = 256
MESH = pl.DeviceIdType.MESH
ORDER = (
    (1, 0), (0, 1), (-1, 0), (0, -1), (1, 1), (-1, -1), (1, -1), (-1, 1),
    (2, 0), (0, 2), (2, 1), (1, 2), (2, -1), (-1, 2), (2, 2),
)
SIDE = 4
F32 = jnp.float32
BF16 = jnp.bfloat16


def mm(a, b):
    return lax.dot_general(a, b, (((1,), (0,)), ((), ())), preferred_element_type=F32)


def mm_nt(a, b):
    return lax.dot_general(a, b, (((1,), (1,)), ((), ())), preferred_element_type=F32)


def mm_tn(a, b):
    return lax.dot_general(a, b, (((0,), (0,)), ((), ())), preferred_element_type=F32)


def kernel(
    scale,
    count,
    early,
    q_hbm,
    k_hbm,
    v_hbm,
    g_hbm,
    dq_ref,
    dk_ref,
    dv_ref,
    q_ref,
    k_ref,
    v_ref,
    g_ref,
    pq_ref,
    pk_ref,
    pv_ref,
    sums,
    parts,
    gathered,
    scans,
    states,
    load_sem,
    send_a,
    recv_a,
    send_b,
    recv_b,
):
    me = lax.axis_index("seq")
    rows = q_ref.shape[0]
    chunks = rows // CHUNK

    def peer(step):
        return lax.rem(me + step, count)

    def toward(dx, dy):
        x = lax.rem(lax.rem(me, SIDE) + dx + SIDE, SIDE)
        y = lax.rem(lax.div(me, SIDE) + dy + SIDE, SIDE)
        return y * SIDE + x

    def lanes(head):
        return pl.ds(pl.multiple_of(head * HEAD_DIM, HEAD_DIM), HEAD_DIM)

    barrier = pltpu.get_barrier_semaphore()

    def greet(step, carry):
        pl.semaphore_signal(barrier, inc=1, device_id={"seq": peer(step)}, device_id_type=MESH)
        return carry

    lax.fori_loop(1, count, greet, 0)

    def pair_at(step):
        return lax.rem(me // 2 + step, HEADS // 2)

    def wide_lanes(pair):
        return pl.ds(pl.multiple_of(pair * 2 * HEAD_DIM, 2 * HEAD_DIM), 2 * HEAD_DIM)

    def load(which, pair):
        source = (k_hbm, v_hbm, q_hbm, g_hbm)[which]
        target = (k_ref, v_ref, q_ref, g_ref)[which]
        return pltpu.make_async_copy(
            source.at[:, wide_lanes(pair)], target.at[:, wide_lanes(pair)], load_sem.at[which, pair]
        )

    for first in (0, 2):

        def begin(step, carry):
            load(first, pair_at(step)).start()
            load(first + 1, pair_at(step)).start()
            return carry

        lax.fori_loop(1, HEADS // 2 + 1, begin, 0)

    def to_hub(kind, head):
        return pltpu.make_async_remote_copy(
            src_ref=sums.at[kind, head],
            dst_ref=gathered.at[kind, me],
            send_sem=send_a.at[kind, head],
            recv_sem=recv_a.at[kind, me],
            device_id={"seq": head},
            device_id_type=MESH,
        )

    def from_source(kind, source):
        return pltpu.make_async_remote_copy(
            src_ref=sums.at[kind, source],
            dst_ref=gathered.at[kind, source],
            send_sem=send_a.at[kind, source],
            recv_sem=recv_a.at[kind, source],
            device_id={"seq": source},
            device_id_type=MESH,
        )

    def to_owner(kind, owner):
        return pltpu.make_async_remote_copy(
            src_ref=scans.at[kind, owner],
            dst_ref=states.at[kind, me],
            send_sem=send_b.at[kind, owner],
            recv_sem=recv_b.at[kind, me],
            device_id={"seq": owner},
            device_id_type=MESH,
        )

    def from_hub(kind, hub):
        return pltpu.make_async_remote_copy(
            src_ref=scans.at[kind, hub],
            dst_ref=states.at[kind, hub],
            send_sem=send_b.at[kind, hub],
            recv_sem=recv_b.at[kind, hub],
            device_id={"seq": hub},
            device_id_type=MESH,
        )

    def reduce_pair(kind, pair):
        left = (k_ref, q_ref)[kind]
        right = (v_ref, g_ref)[kind]
        load(2 * kind, pair).wait()
        load(2 * kind + 1, pair).wait()
        total = None
        for step in range(chunks):
            chunk = step if kind == 0 else chunks - 1 - step
            here = pl.ds(chunk * CHUNK, CHUNK)
            both = mm_tn(left[here, wide_lanes(pair)], right[here, wide_lanes(pair)])
            term = (both[:HEAD_DIM, :HEAD_DIM], both[HEAD_DIM:, HEAD_DIM:])
            total = term if total is None else (total[0] + term[0], total[1] + term[1])
            for one in (0, 1):
                if step < chunks - 1:
                    parts[kind, step, 2 * pair + one] = total[one]
                else:
                    sums[kind, 2 * pair + one] = total[one]

    for kind in (0, 1):

        def add_pair(step, carry):
            reduce_pair(kind, pair_at(step))
            return carry

        lax.fori_loop(1, HEADS // 2 + 1, add_pair, 0)
        if kind == 0:
            pl.semaphore_wait(barrier, count - 1)
        for dx, dy in ORDER:
            to_hub(kind, toward(dx, dy)).start()
        gathered[kind, me] = sums[kind, me]

    later = lax.broadcasted_iota(jnp.int32, (CHUNK, CHUNK), 0)
    sooner = lax.broadcasted_iota(jnp.int32, (CHUNK, CHUNK), 1)

    def within(head, carry):
        for chunk in range(chunks):
            here = pl.ds(chunk * CHUNK, CHUNK)
            q = q_ref[here, lanes(head)]
            k = k_ref[here, lanes(head)]
            v = v_ref[here, lanes(head)]
            g = g_ref[here, lanes(head)]
            weights = jnp.where(later >= sooner, scale * mm_nt(g, v), 0.0).astype(BF16)
            pq_ref[here, lanes(head)] = mm(weights, k)
            turned = jnp.where(later <= sooner, scale * mm_nt(v, g), 0.0).astype(BF16)
            pk_ref[here, lanes(head)] = mm(turned, q)
            forward = jnp.where(later <= sooner, scale * mm_nt(k, q), 0.0).astype(BF16)
            pv_ref[here, lanes(head)] = mm(forward, g)
        return carry

    def scan(kind):
        def arrive(step, carry):
            from_source(kind, peer(step)).wait_recv()
            return carry

        lax.fori_loop(1, count, arrive, 0)

        def add(step, carry):
            source = step if kind == 0 else count - 1 - step
            scans[kind, source] = carry
            return carry + gathered[kind, source]

        lax.fori_loop(0, count, add, jnp.zeros((HEAD_DIM, HEAD_DIM), F32))
        states[kind, me] = scans[kind, me]

        for dx, dy in ORDER:
            to_owner(kind, toward(dx, dy)).start()

    lax.fori_loop(0, early, within, 0)
    scan(0)
    lax.fori_loop(early, HEADS, within, 0)
    scan(1)

    def state_at(kind, head, step):
        state = states[kind, head]
        if step > 0:
            state = state + parts[kind, step - 1, head]
        return state.astype(BF16)

    def finish_q(head):
        for chunk in range(chunks):
            here = pl.ds(chunk * CHUNK, CHUNK)
            carried = mm_nt(g_ref[here, lanes(head)], state_at(0, head, chunk))
            dq_ref[here, lanes(head)] = (pq_ref[here, lanes(head)] + scale * carried).astype(BF16)

    def finish_kv(head):
        for chunk in range(chunks):
            here = pl.ds(chunk * CHUNK, CHUNK)
            state = state_at(1, head, chunks - 1 - chunk)
            carried = mm_nt(v_ref[here, lanes(head)], state)
            dk_ref[here, lanes(head)] = (pk_ref[here, lanes(head)] + scale * carried).astype(BF16)
            carried = mm(k_ref[here, lanes(head)], state)
            dv_ref[here, lanes(head)] = (pv_ref[here, lanes(head)] + scale * carried).astype(BF16)

    for kind, finish in ((0, finish_q), (1, finish_kv)):
        finish(me)

        for dx, dy in ORDER:
            head = toward(-dx, -dy)
            from_hub(kind, head).wait_recv()
            finish(head)

    for kind in (0, 1):
        for dx, dy in ORDER:
            to_hub(kind, toward(dx, dy)).wait_send()
        for dx, dy in ORDER:
            to_owner(kind, toward(dx, dy)).wait_send()


def store_kernel(dq_ref, dk_ref, dv_ref, dq_hbm, dk_hbm, dv_hbm, sems):
    copies = []
    for i, (source, target) in enumerate(
        ((dq_ref, dq_hbm), (dk_ref, dk_hbm), (dv_ref, dv_hbm))
    ):
        copies.append(pltpu.make_async_copy(source, target, sems.at[i]))
    for copy in copies:
        copy.start()
    for copy in copies:
        copy.wait()


def on_device(queries, key_rows, value_rows, out_grad):
    rows, width = queries.shape
    count = lax.axis_size("seq")
    scale = (HEAD_DIM * rows * count) ** (-0.5)
    wide = (rows, width)
    square = (HEAD_DIM, HEAD_DIM)
    chunks = rows // CHUNK
    grads = pl.pallas_call(
        functools.partial(kernel, scale, count, 10),
        name="layer",
        out_shape=[pltpu.VMEM(wide, BF16)] * 3,
        in_specs=[pl.BlockSpec(memory_space=pl.ANY)] * 4,
        out_specs=[pl.BlockSpec(memory_space=pltpu.VMEM)] * 3,
        scratch_shapes=[pltpu.VMEM(wide, BF16)] * 4
        + [pltpu.VMEM(wide, F32)] * 3
        + [
            pltpu.VMEM((2, HEADS) + square, F32),
            pltpu.VMEM((2, chunks - 1, HEADS) + square, F32),
            pltpu.VMEM((2, count) + square, F32),
            pltpu.VMEM((2, count) + square, F32),
            pltpu.VMEM((2, HEADS) + square, F32),
            pltpu.SemaphoreType.DMA((4, HEADS)),
            pltpu.SemaphoreType.DMA((2, HEADS)),
            pltpu.SemaphoreType.DMA((2, count)),
            pltpu.SemaphoreType.DMA((2, count)),
            pltpu.SemaphoreType.DMA((2, HEADS)),
        ],
        compiler_params=pltpu.CompilerParams(
            collective_id=0, has_side_effects=True, vmem_limit_bytes=48 << 20
        ),
    )(queries, key_rows, value_rows, out_grad)
    return pl.pallas_call(
        store_kernel,
        name="store",
        out_shape=[jax.ShapeDtypeStruct(wide, BF16)] * 3,
        in_specs=[pl.BlockSpec(memory_space=pltpu.VMEM)] * 3,
        out_specs=[pl.BlockSpec(memory_space=pl.ANY)] * 3,
        scratch_shapes=[pltpu.SemaphoreType.DMA((3,))],
        compiler_params=pltpu.CompilerParams(vmem_limit_bytes=1 << 20),
    )(*grads)


def solution(mesh):
    placed = P(("lists", "seq"), None)
    return jax.shard_map(
        on_device,
        mesh=mesh,
        in_specs=(placed,) * 4,
        out_specs=(placed,) * 3,
        check_vma=False,
    )
```

```python
import functools

import jax
import jax.numpy as jnp
from jax import lax
from jax.experimental import pallas as pl
from jax.experimental.pallas import tpu as pltpu
from jax.sharding import PartitionSpec as P

HEADS = 16
HEAD_DIM = 128
CHUNK = 256
MESH = pl.DeviceIdType.MESH
ORDER = (
    (1, 0), (0, 1), (-1, 0), (0, -1), (1, 1), (-1, -1), (1, -1), (-1, 1),
    (2, 0), (0, 2), (2, 1), (1, 2), (2, -1), (-1, 2), (2, 2),
)
SIDE = 4
PIECES = 4
F32 = jnp.float32
BF16 = jnp.bfloat16


def mm(a, b):
    return lax.dot_general(a, b, (((1,), (0,)), ((), ())), preferred_element_type=F32)


def mm_nt(a, b):
    return lax.dot_general(a, b, (((1,), (1,)), ((), ())), preferred_element_type=F32)


def mm_tn(a, b):
    return lax.dot_general(a, b, (((0,), (0,)), ((), ())), preferred_element_type=F32)


def kernel(
    scale,
    count,
    early,
    q_hbm,
    k_hbm,
    v_hbm,
    g_hbm,
    dq_ref,
    dk_ref,
    dv_ref,
    q_ref,
    k_ref,
    v_ref,
    g_ref,
    pq_ref,
    pk_ref,
    pv_ref,
    sums,
    parts,
    gathered,
    scans,
    states,
    load_sem,
    send_a,
    recv_a,
    send_b,
    recv_b,
):
    me = lax.axis_index("seq")
    rows = q_ref.shape[0]
    chunks = rows // CHUNK

    def peer(step):
        return lax.rem(me + step, count)

    def toward(dx, dy):
        x = lax.rem(lax.rem(me, SIDE) + dx + SIDE, SIDE)
        y = lax.rem(lax.div(me, SIDE) + dy + SIDE, SIDE)
        return y * SIDE + x

    def lanes(head):
        return pl.ds(pl.multiple_of(head * HEAD_DIM, HEAD_DIM), HEAD_DIM)

    barrier = pltpu.get_barrier_semaphore()

    def greet(step, carry):
        pl.semaphore_signal(barrier, inc=1, device_id={"seq": peer(step)}, device_id_type=MESH)
        return carry

    lax.fori_loop(1, count, greet, 0)

    def pair_at(step):
        return lax.rem(me // 2 + step, HEADS // 2)

    def wide_lanes(pair):
        return pl.ds(pl.multiple_of(pair * 2 * HEAD_DIM, 2 * HEAD_DIM), 2 * HEAD_DIM)

    def load(which, pair):
        source = (k_hbm, v_hbm, q_hbm, g_hbm)[which]
        target = (k_ref, v_ref, q_ref, g_ref)[which]
        return pltpu.make_async_copy(
            source.at[:, wide_lanes(pair)], target.at[:, wide_lanes(pair)], load_sem.at[which, pair]
        )

    for first in (0, 2):

        def begin(step, carry):
            load(first, pair_at(step)).start()
            load(first + 1, pair_at(step)).start()
            return carry

        lax.fori_loop(1, HEADS // 2 + 1, begin, 0)

    def to_hub(kind, head):
        return pltpu.make_async_remote_copy(
            src_ref=sums.at[kind, head],
            dst_ref=gathered.at[kind, me],
            send_sem=send_a.at[kind, head],
            recv_sem=recv_a.at[kind, me],
            device_id={"seq": head},
            device_id_type=MESH,
        )

    def from_source(kind, source):
        return pltpu.make_async_remote_copy(
            src_ref=sums.at[kind, source],
            dst_ref=gathered.at[kind, source],
            send_sem=send_a.at[kind, source],
            recv_sem=recv_a.at[kind, source],
            device_id={"seq": source},
            device_id_type=MESH,
        )

    def to_owner(kind, owner):
        return pltpu.make_async_remote_copy(
            src_ref=scans.at[kind, owner],
            dst_ref=states.at[kind, me],
            send_sem=send_b.at[kind, owner],
            recv_sem=recv_b.at[kind, me],
            device_id={"seq": owner},
            device_id_type=MESH,
        )

    def from_hub(kind, hub):
        return pltpu.make_async_remote_copy(
            src_ref=scans.at[kind, hub],
            dst_ref=states.at[kind, hub],
            send_sem=send_b.at[kind, hub],
            recv_sem=recv_b.at[kind, hub],
            device_id={"seq": hub},
            device_id_type=MESH,
        )

    def reduce_pair(kind, pair):
        left = (k_ref, q_ref)[kind]
        right = (v_ref, g_ref)[kind]
        load(2 * kind, pair).wait()
        load(2 * kind + 1, pair).wait()
        total = None
        for step in range(chunks):
            chunk = step if kind == 0 else chunks - 1 - step
            here = pl.ds(chunk * CHUNK, CHUNK)
            both = mm_tn(left[here, wide_lanes(pair)], right[here, wide_lanes(pair)])
            term = (both[:HEAD_DIM, :HEAD_DIM], both[HEAD_DIM:, HEAD_DIM:])
            total = term if total is None else (total[0] + term[0], total[1] + term[1])
            for one in (0, 1):
                if step < chunks - 1:
                    parts[kind, step, 2 * pair + one] = total[one]
                else:
                    sums[kind, 2 * pair + one] = total[one]

    for kind in (0, 1):

        def add_pair(step, carry):
            reduce_pair(kind, pair_at(step))
            return carry

        lax.fori_loop(1, HEADS // 2 + 1, add_pair, 0)
        if kind == 0:
            pl.semaphore_wait(barrier, count - 1)
        for dx, dy in ORDER:
            to_hub(kind, toward(dx, dy)).start()
        gathered[kind, me] = sums[kind, me]

    later = lax.broadcasted_iota(jnp.int32, (CHUNK, CHUNK), 0)
    sooner = lax.broadcasted_iota(jnp.int32, (CHUNK, CHUNK), 1)

    def within(head, carry):
        for chunk in range(chunks):
            here = pl.ds(chunk * CHUNK, CHUNK)
            q = q_ref[here, lanes(head)]
            k = k_ref[here, lanes(head)]
            v = v_ref[here, lanes(head)]
            g = g_ref[here, lanes(head)]
            weights = jnp.where(later >= sooner, scale * mm_nt(g, v), 0.0).astype(BF16)
            pq_ref[here, lanes(head)] = mm(weights, k)
            turned = jnp.where(later <= sooner, scale * mm_nt(v, g), 0.0).astype(BF16)
            pk_ref[here, lanes(head)] = mm(turned, q)
            forward = jnp.where(later <= sooner, scale * mm_nt(k, q), 0.0).astype(BF16)
            pv_ref[here, lanes(head)] = mm(forward, g)
        return carry

    def scan(kind):
        def arrive(step, carry):
            from_source(kind, peer(step)).wait_recv()
            return carry

        lax.fori_loop(1, count, arrive, 0)

        def add(step, carry):
            source = step if kind == 0 else count - 1 - step
            scans[kind, source] = carry
            return carry + gathered[kind, source]

        lax.fori_loop(0, count, add, jnp.zeros((HEAD_DIM, HEAD_DIM), F32))
        states[kind, me] = scans[kind, me]

        for dx, dy in ORDER:
            to_owner(kind, toward(dx, dy)).start()

    lax.fori_loop(0, early, within, 0)
    scan(0)
    lax.fori_loop(early, HEADS, within, 0)
    scan(1)

    def state_at(kind, head, step):
        state = states[kind, head]
        if step > 0:
            state = state + parts[kind, step - 1, head]
        return state.astype(BF16)

    def finish_q(head):
        for chunk in range(chunks):
            here = pl.ds(chunk * CHUNK, CHUNK)
            carried = mm_nt(g_ref[here, lanes(head)], state_at(0, head, chunk))
            dq_ref[here, lanes(head)] = (pq_ref[here, lanes(head)] + scale * carried).astype(BF16)

    def finish_kv(head):
        for chunk in range(chunks):
            here = pl.ds(chunk * CHUNK, CHUNK)
            state = state_at(1, head, chunks - 1 - chunk)
            carried = mm_nt(v_ref[here, lanes(head)], state)
            dk_ref[here, lanes(head)] = (pk_ref[here, lanes(head)] + scale * carried).astype(BF16)
            carried = mm(k_ref[here, lanes(head)], state)
            dv_ref[here, lanes(head)] = (pv_ref[here, lanes(head)] + scale * carried).astype(BF16)

    for kind, finish in ((0, finish_q), (1, finish_kv)):
        finish(me)

        for dx, dy in ORDER:
            head = toward(-dx, -dy)
            from_hub(kind, head).wait_recv()
            finish(head)

    for kind in (0, 1):
        for dx, dy in ORDER:
            to_hub(kind, toward(dx, dy)).wait_send()
        for dx, dy in ORDER:
            to_owner(kind, toward(dx, dy)).wait_send()


def store_kernel(dq_ref, dk_ref, dv_ref, dq_hbm, dk_hbm, dv_hbm, sems):
    copies = []
    for i, (source, target) in enumerate(
        ((dq_ref, dq_hbm), (dk_ref, dk_hbm), (dv_ref, dv_hbm))
    ):
        for j in range(PIECES):
            block = source.shape[0] // PIECES
            piece = pl.ds(j * block, block)
            copies.append(
                pltpu.make_async_copy(source.at[piece], target.at[piece], sems.at[i, j])
            )
    for copy in copies:
        copy.start()
    for copy in copies:
        copy.wait()


def on_device(queries, key_rows, value_rows, out_grad):
    rows, width = queries.shape
    count = lax.axis_size("seq")
    scale = (HEAD_DIM * rows * count) ** (-0.5)
    wide = (rows, width)
    square = (HEAD_DIM, HEAD_DIM)
    chunks = rows // CHUNK
    grads = pl.pallas_call(
        functools.partial(kernel, scale, count, 10),
        name="layer",
        out_shape=[pltpu.VMEM(wide, BF16)] * 3,
        in_specs=[pl.BlockSpec(memory_space=pl.ANY)] * 4,
        out_specs=[pl.BlockSpec(memory_space=pltpu.VMEM)] * 3,
        scratch_shapes=[pltpu.VMEM(wide, BF16)] * 4
        + [pltpu.VMEM(wide, F32)] * 3
        + [
            pltpu.VMEM((2, HEADS) + square, F32),
            pltpu.VMEM((2, chunks - 1, HEADS) + square, F32),
            pltpu.VMEM((2, count) + square, F32),
            pltpu.VMEM((2, count) + square, F32),
            pltpu.VMEM((2, HEADS) + square, F32),
            pltpu.SemaphoreType.DMA((4, HEADS)),
            pltpu.SemaphoreType.DMA((2, HEADS)),
            pltpu.SemaphoreType.DMA((2, count)),
            pltpu.SemaphoreType.DMA((2, count)),
            pltpu.SemaphoreType.DMA((2, HEADS)),
        ],
        compiler_params=pltpu.CompilerParams(
            collective_id=0, has_side_effects=True, vmem_limit_bytes=48 << 20
        ),
    )(queries, key_rows, value_rows, out_grad)
    return pl.pallas_call(
        store_kernel,
        name="store",
        out_shape=[jax.ShapeDtypeStruct(wide, BF16)] * 3,
        in_specs=[pl.BlockSpec(memory_space=pltpu.VMEM)] * 3,
        out_specs=[pl.BlockSpec(memory_space=pl.ANY)] * 3,
        scratch_shapes=[pltpu.SemaphoreType.DMA((3, PIECES))],
        compiler_params=pltpu.CompilerParams(vmem_limit_bytes=1 << 20),
    )(*grads)


def solution(mesh):
    placed = P(("lists", "seq"), None)
    return jax.shard_map(
        on_device,
        mesh=mesh,
        in_specs=(placed,) * 4,
        out_specs=(placed,) * 3,
        check_vma=False,
    )
```

```python
import functools

import jax
import jax.numpy as jnp
from jax import lax
from jax.experimental import pallas as pl
from jax.experimental.pallas import tpu as pltpu
from jax.sharding import PartitionSpec as P

HEADS = 16
HEAD_DIM = 128
CHUNK = 256
MESH = pl.DeviceIdType.MESH
ORDER = (
    (1, 0), (0, 1), (-1, 0), (0, -1), (1, 1), (-1, -1), (1, -1), (-1, 1),
    (2, 0), (0, 2), (2, 1), (1, 2), (2, -1), (-1, 2), (2, 2),
)
SIDE = 4
PIECES = 4
F32 = jnp.float32
BF16 = jnp.bfloat16


def mm(a, b):
    return lax.dot_general(a, b, (((1,), (0,)), ((), ())), preferred_element_type=F32)


def mm_nt(a, b):
    return lax.dot_general(a, b, (((1,), (1,)), ((), ())), preferred_element_type=F32)


def mm_tn(a, b):
    return lax.dot_general(a, b, (((0,), (0,)), ((), ())), preferred_element_type=F32)


def kernel(
    scale,
    count,
    early,
    q_hbm,
    k_hbm,
    v_hbm,
    g_hbm,
    dq_ref,
    dk_ref,
    dv_ref,
    q_ref,
    k_ref,
    v_ref,
    g_ref,
    pq_ref,
    pk_ref,
    pv_ref,
    sums,
    parts,
    gathered,
    scans,
    states,
    load_sem,
    send_a,
    recv_a,
    send_b,
    recv_b,
):
    me = lax.axis_index("seq")
    rows = q_ref.shape[0]
    chunks = rows // CHUNK

    def peer(step):
        return lax.rem(me + step, count)

    def unused(kind):
        return count - 1 if kind == 0 else 0

    def toward(dx, dy):
        x = lax.rem(lax.rem(me, SIDE) + dx + SIDE, SIDE)
        y = lax.rem(lax.div(me, SIDE) + dy + SIDE, SIDE)
        return y * SIDE + x

    def lanes(head):
        return pl.ds(pl.multiple_of(head * HEAD_DIM, HEAD_DIM), HEAD_DIM)

    barrier = pltpu.get_barrier_semaphore()

    def greet(step, carry):
        pl.semaphore_signal(barrier, inc=1, device_id={"seq": peer(step)}, device_id_type=MESH)
        return carry

    lax.fori_loop(1, count, greet, 0)

    def pair_at(step):
        return lax.rem(me // 2 + step, HEADS // 2)

    def wide_lanes(pair):
        return pl.ds(pl.multiple_of(pair * 2 * HEAD_DIM, 2 * HEAD_DIM), 2 * HEAD_DIM)

    def load(which, pair):
        source = (k_hbm, v_hbm, q_hbm, g_hbm)[which]
        target = (k_ref, v_ref, q_ref, g_ref)[which]
        return pltpu.make_async_copy(
            source.at[:, wide_lanes(pair)], target.at[:, wide_lanes(pair)], load_sem.at[which, pair]
        )

    for first in (0, 2):

        def begin(step, carry):
            load(first, pair_at(step)).start()
            load(first + 1, pair_at(step)).start()
            return carry

        lax.fori_loop(1, HEADS // 2 + 1, begin, 0)

    def to_hub(kind, head):
        return pltpu.make_async_remote_copy(
            src_ref=sums.at[kind, head],
            dst_ref=gathered.at[kind, me],
            send_sem=send_a.at[kind, head],
            recv_sem=recv_a.at[kind, me],
            device_id={"seq": head},
            device_id_type=MESH,
        )

    def from_source(kind, source):
        return pltpu.make_async_remote_copy(
            src_ref=sums.at[kind, source],
            dst_ref=gathered.at[kind, source],
            send_sem=send_a.at[kind, source],
            recv_sem=recv_a.at[kind, source],
            device_id={"seq": source},
            device_id_type=MESH,
        )

    def to_owner(kind, owner):
        return pltpu.make_async_remote_copy(
            src_ref=scans.at[kind, owner],
            dst_ref=states.at[kind, me],
            send_sem=send_b.at[kind, owner],
            recv_sem=recv_b.at[kind, me],
            device_id={"seq": owner},
            device_id_type=MESH,
        )

    def from_hub(kind, hub):
        return pltpu.make_async_remote_copy(
            src_ref=scans.at[kind, hub],
            dst_ref=states.at[kind, hub],
            send_sem=send_b.at[kind, hub],
            recv_sem=recv_b.at[kind, hub],
            device_id={"seq": hub},
            device_id_type=MESH,
        )

    def reduce_pair(kind, pair):
        left = (k_ref, q_ref)[kind]
        right = (v_ref, g_ref)[kind]
        load(2 * kind, pair).wait()
        load(2 * kind + 1, pair).wait()
        total = None
        for step in range(chunks):
            chunk = step if kind == 0 else chunks - 1 - step
            here = pl.ds(chunk * CHUNK, CHUNK)
            both = mm_tn(left[here, wide_lanes(pair)], right[here, wide_lanes(pair)])
            term = (both[:HEAD_DIM, :HEAD_DIM], both[HEAD_DIM:, HEAD_DIM:])
            total = term if total is None else (total[0] + term[0], total[1] + term[1])
            for one in (0, 1):
                if step < chunks - 1:
                    parts[kind, step, 2 * pair + one] = total[one]
                else:
                    sums[kind, 2 * pair + one] = total[one]

    for kind in (0, 1):

        def add_pair(step, carry):
            reduce_pair(kind, pair_at(step))
            return carry

        lax.fori_loop(1, HEADS // 2 + 1, add_pair, 0)
        if kind == 0:
            pl.semaphore_wait(barrier, count - 1)

        @pl.when(me != unused(kind))
        def _():
            for dx, dy in ORDER:
                to_hub(kind, toward(dx, dy)).start()

        gathered[kind, me] = sums[kind, me]

        @pl.when(me == unused(1 - kind))
        def _():
            for head in range(HEADS):
                states[kind, head] = jnp.zeros((HEAD_DIM, HEAD_DIM), F32)


    later = lax.broadcasted_iota(jnp.int32, (CHUNK, CHUNK), 0)
    sooner = lax.broadcasted_iota(jnp.int32, (CHUNK, CHUNK), 1)

    def within(head, carry):
        for chunk in range(chunks):
            here = pl.ds(chunk * CHUNK, CHUNK)
            q = q_ref[here, lanes(head)]
            k = k_ref[here, lanes(head)]
            v = v_ref[here, lanes(head)]
            g = g_ref[here, lanes(head)]
            weights = jnp.where(later >= sooner, scale * mm_nt(g, v), 0.0).astype(BF16)
            pq_ref[here, lanes(head)] = mm(weights, k)
            turned = jnp.where(later <= sooner, scale * mm_nt(v, g), 0.0).astype(BF16)
            pk_ref[here, lanes(head)] = mm(turned, q)
            forward = jnp.where(later <= sooner, scale * mm_nt(k, q), 0.0).astype(BF16)
            pv_ref[here, lanes(head)] = mm(forward, g)
        return carry

    def scan(kind):
        def arrive(step, carry):
            source = peer(step)

            @pl.when(source != unused(kind))
            def _():
                from_source(kind, source).wait_recv()

            return carry

        lax.fori_loop(1, count, arrive, 0)

        def add(step, carry):
            source = step if kind == 0 else count - 1 - step
            scans[kind, source] = carry
            return carry + gathered[kind, source]

        total = lax.fori_loop(0, count - 1, add, jnp.zeros((HEAD_DIM, HEAD_DIM), F32))
        scans[kind, unused(kind)] = total
        states[kind, me] = scans[kind, me]

        for dx, dy in ORDER:

            @pl.when(toward(dx, dy) != unused(1 - kind))
            def _():
                to_owner(kind, toward(dx, dy)).start()


    lax.fori_loop(0, early, within, 0)
    scan(0)
    lax.fori_loop(early, HEADS, within, 0)
    scan(1)

    def state_at(kind, head, step):
        state = states[kind, head]
        if step > 0:
            state = state + parts[kind, step - 1, head]
        return state.astype(BF16)

    def finish_q(head):
        for chunk in range(chunks):
            here = pl.ds(chunk * CHUNK, CHUNK)
            carried = mm_nt(g_ref[here, lanes(head)], state_at(0, head, chunk))
            dq_ref[here, lanes(head)] = (pq_ref[here, lanes(head)] + scale * carried).astype(BF16)

    def finish_kv(head):
        for chunk in range(chunks):
            here = pl.ds(chunk * CHUNK, CHUNK)
            state = state_at(1, head, chunks - 1 - chunk)
            carried = mm_nt(v_ref[here, lanes(head)], state)
            dk_ref[here, lanes(head)] = (pk_ref[here, lanes(head)] + scale * carried).astype(BF16)
            carried = mm(k_ref[here, lanes(head)], state)
            dv_ref[here, lanes(head)] = (pv_ref[here, lanes(head)] + scale * carried).astype(BF16)

    for kind, finish in ((0, finish_q), (1, finish_kv)):
        finish(me)

        for dx, dy in ORDER:
            head = toward(-dx, -dy)

            @pl.when(me != unused(1 - kind))
            def _():
                from_hub(kind, head).wait_recv()

            finish(head)

    for kind in (0, 1):

        @pl.when(me != unused(kind))
        def _():
            for dx, dy in ORDER:
                to_hub(kind, toward(dx, dy)).wait_send()

        for dx, dy in ORDER:

            @pl.when(toward(dx, dy) != unused(1 - kind))
            def _():
                to_owner(kind, toward(dx, dy)).wait_send()


def store_kernel(dq_ref, dk_ref, dv_ref, dq_hbm, dk_hbm, dv_hbm, sems):
    copies = []
    for i, (source, target) in enumerate(
        ((dq_ref, dq_hbm), (dk_ref, dk_hbm), (dv_ref, dv_hbm))
    ):
        for j in range(PIECES):
            block = source.shape[0] // PIECES
            piece = pl.ds(j * block, block)
            copies.append(
                pltpu.make_async_copy(source.at[piece], target.at[piece], sems.at[i, j])
            )
    for copy in copies:
        copy.start()
    for copy in copies:
        copy.wait()


def on_device(queries, key_rows, value_rows, out_grad):
    rows, width = queries.shape
    count = lax.axis_size("seq")
    scale = (HEAD_DIM * rows * count) ** (-0.5)
    wide = (rows, width)
    square = (HEAD_DIM, HEAD_DIM)
    chunks = rows // CHUNK
    grads = pl.pallas_call(
        functools.partial(kernel, scale, count, 10),
        name="layer",
        out_shape=[pltpu.VMEM(wide, BF16)] * 3,
        in_specs=[pl.BlockSpec(memory_space=pl.ANY)] * 4,
        out_specs=[pl.BlockSpec(memory_space=pltpu.VMEM)] * 3,
        scratch_shapes=[pltpu.VMEM(wide, BF16)] * 4
        + [pltpu.VMEM(wide, F32)] * 3
        + [
            pltpu.VMEM((2, HEADS) + square, F32),
            pltpu.VMEM((2, chunks - 1, HEADS) + square, F32),
            pltpu.VMEM((2, count) + square, F32),
            pltpu.VMEM((2, count) + square, F32),
            pltpu.VMEM((2, HEADS) + square, F32),
            pltpu.SemaphoreType.DMA((4, HEADS)),
            pltpu.SemaphoreType.DMA((2, HEADS)),
            pltpu.SemaphoreType.DMA((2, count)),
            pltpu.SemaphoreType.DMA((2, count)),
            pltpu.SemaphoreType.DMA((2, HEADS)),
        ],
        compiler_params=pltpu.CompilerParams(
            collective_id=0, has_side_effects=True, vmem_limit_bytes=48 << 20
        ),
    )(queries, key_rows, value_rows, out_grad)
    return pl.pallas_call(
        store_kernel,
        name="store",
        out_shape=[jax.ShapeDtypeStruct(wide, BF16)] * 3,
        in_specs=[pl.BlockSpec(memory_space=pltpu.VMEM)] * 3,
        out_specs=[pl.BlockSpec(memory_space=pl.ANY)] * 3,
        scratch_shapes=[pltpu.SemaphoreType.DMA((3, PIECES))],
        compiler_params=pltpu.CompilerParams(vmem_limit_bytes=1 << 20),
    )(*grads)


def solution(mesh):
    placed = P(("lists", "seq"), None)
    return jax.shard_map(
        on_device,
        mesh=mesh,
        in_specs=(placed,) * 4,
        out_specs=(placed,) * 3,
        check_vma=False,
    )
```
